32 devices in a mesh: cube: 4 (over y, x), panel: 8 (over z, core).
Axes of the slice: x: 2, y: 2, z: 4, core: 2. Of those that a mesh axis runs over, the one named last changes fastest.
Arguments:
- columns: bfloat16 [96, 4, 4096], P('cube', None, 'panel'), may hold values from -8 to 8
- leaf_of: int32 [96, 1], P('cube'), may hold values from 0 to 3; in each aligned block of 24 rows (0 to 23, 24 to 47, ...) at most 12 rows name the same one
- inverse_root: bfloat16 [4096, 4096], P('cube', 'panel'), may hold values from -0.5 to 0.5, as said below
- inverse_upper: bfloat16 [8192, 4096], P('cube', 'panel'), may hold values from -0.5 to 0.5, as said below
- inverse_middle: bfloat16 [16384, 4096], P('cube', 'panel'), may hold values from -0.5 to 0.5, as said below
- inverse_leaf: bfloat16 [16384, 4096], P('cube', 'panel'), may hold values from -0.5 to 0.5, as said below
- coupling_upper: bfloat16 [8192, 1, 4096], P('cube', None, 'panel'), may hold values from -6 to 6
- coupling_middle: bfloat16 [16384, 2, 4096], P('cube', None, 'panel'), may hold values from -6 to 6
- coupling_leaf: bfloat16 [16384, 3, 4096], P('cube', None, 'panel'), may hold values from -6 to 6
Outputs:
- core_factor: float32 [192, 192], replicated
- project_root: bfloat16 [4096, 192], P(('cube', 'panel'))
- project_upper: bfloat16 [8192, 96], P(('cube', 'panel'))
- project_middle: bfloat16 [16384, 48], P(('cube', 'panel'))
- project_leaf: bfloat16 [16384, 48], P(('cube', 'panel'))
The draws below stay inside these ranges and needn't reach their ends.
Inputs may be any that keep to these rules, and one draw needn't show every extreme that they name: `leaf_of`: among the 24 columns held by one index of cube, no leaf is named more than 12 times. `inverse_root`: each block of 4096 rows is lower triangular. `inverse_upper`: each block of 4096 rows is lower triangular. `inverse_middle`: each block of 4096 rows is lower triangular. `inverse_leaf`: each block of 4096 rows is lower triangular.
All inputs are finite; a program needn't handle non-finite values.
Results may differ from the reference program's by a relative error of at most 0.011.
Values may be sent and summed in bfloat16 or wider, within the bound.
A program may use at most 128 MiB of HBM per device.

```python
import math
import jax
import jax.numpy as jnp
import numpy as np

NS = 4096
TIME_DEV = 24
RANK = 96
LEAVES = 4
MIDDLE_NODES = 4
UPPER_NODES = 2
LEAF_SPAN = 1
M = 12
PER_SLOT = 12
C_DEV = 48
FRONT = 192
N_CUBE = 4


def draw_columns(key, part):
    key_noise, key_common, key_weight = jax.random.split(key, 3)
    noise = jnp.clip(jax.random.normal(key_noise, (RANK, 4, NS), jnp.float32), -5.0, 5.0)
    common = jnp.clip(jax.random.normal(key_common, (4, NS), jnp.float32), -5.0, 5.0)
    weights = jax.random.uniform(key_weight, (RANK,), jnp.float32, -1.0, 1.0)
    values = 0.8 * noise + 0.6 * weights[:, None, None] * common[None]
    return values.astype(jnp.bfloat16)


def lower_blocks(key, nodes, label):
    key_spread, key_diag = jax.random.split(jax.random.fold_in(key, label))
    row_pos = jnp.arange(nodes * NS, dtype=jnp.int32)[:, None] % NS
    col_pos = jnp.arange(NS, dtype=jnp.int32)[None, :]
    spread = jnp.clip(jax.random.normal(key_spread, (nodes * NS, NS), jnp.float32), -5.0, 5.0)
    diagonal = jnp.exp(jax.random.uniform(key_diag, (nodes * NS, 1), jnp.float32, math.log(0.5), math.log(2.0)))
    values = jnp.where(col_pos < row_pos, spread / NS, jnp.where(col_pos == row_pos, diagonal / math.sqrt(NS), 0.0))
    return values.astype(jnp.bfloat16)


def draw_inverse_root(key, part):
    return lower_blocks(key, 1, 11)


def draw_inverse_upper(key, part):
    return lower_blocks(key, UPPER_NODES, 13)


def draw_inverse_middle(key, part):
    return lower_blocks(key, MIDDLE_NODES, 17)


def draw_inverse_leaf(key, part):
    return lower_blocks(key, LEAVES, 19)


def block_levels(own_key, dims, cuts, smallest, high):
    def one(axis_at, blocks):
        draws = jax.random.uniform(jax.random.fold_in(jax.random.fold_in(own_key, 6), axis_at), (blocks,), jnp.float32, smallest / len(cuts), high / len(cuts))
        return jnp.repeat(jnp.exp(draws), dims[axis_at] // blocks).reshape((-1,) + (1,) * (len(dims) - axis_at - 1))

    gain = one(*cuts[0])
    for cut in cuts[1:]:
        gain = gain * one(*cut)
    return gain


def deal_out(key, own, number, rows, number_of, top, reach, skew):
    sequence = jax.random.permutation(key, number_of)
    packed, usual = portions_of(number_of, rows * top, reach, skew, True), portions_of(number_of, rows * top, reach, skew, False)
    places = jnp.arange(number_of)

    def named(lengths, turn):
        used = int((lengths > 0).sum())
        fixed = max(1, used // 4)
        passed = fixed + (places - fixed + turn * (used - fixed)) % max(1, number_of - fixed)
        return jnp.zeros((number_of,), jnp.int32).at[sequence[jnp.where(places < fixed, places, passed)]].set(jnp.asarray(lengths, jnp.int32))

    lengths = jnp.where(number % 4 == 0, named(packed, number // 4), named(usual, number - number // 4 - 1))
    mixed = jax.random.permutation(jax.random.fold_in(own, 3), number_of)
    donor, sink = mixed[0:number_of // 2 * 2:2], mixed[1:number_of // 2 * 2:2]
    margin = jnp.minimum(lengths[donor] - 1, reach - lengths[sink]) // 2
    margin = jnp.where((donor == sequence[0]) | (sink == sequence[0]) | (lengths[sink] == 0), 0, jnp.maximum(margin, 0))
    passed = jax.random.randint(jax.random.fold_in(own, 4), (number_of // 2,), 0, 1 << 20) % (margin + 1)
    lengths = lengths.at[donor].add(-passed).at[sink].add(passed)
    items = jnp.searchsorted(jnp.cumsum(lengths), jnp.arange(rows * top), side="right").astype(jnp.int32)
    listing = items.reshape(top, rows).T
    listing = listing[jax.random.permutation(jax.random.fold_in(own, 1), rows)]
    turn = jax.random.randint(jax.random.fold_in(own, 2), (rows, 1), 0, top)
    return jnp.take_along_axis(listing, (jnp.arange(top)[None, :] + turn) % top, axis=1)


def portions_of(count, total, limit, slope, full):
    loads = [(1 << 20) // math.isqrt(standing ** slope) + 1 for standing in range(1, count + 1)]
    largest = limit if full else min(limit, max(-(-total // count), total * loads[0] // sum(loads)))
    least = 1 if total - largest >= count - 1 else 0
    given, spare = [largest] + [least] * (count - 1), total - largest - least * (count - 1)
    while spare > 0:
        free = [i for i in range(1, count) if given[i] < largest] or [i for i in range(1, count) if given[i] < limit]
        whole, budget = sum([loads[i] for i in free]), spare
        for i in free:
            more = min(limit - given[i], max(1, budget * loads[i] // whole), spare)
            given[i] = given[i] + more
            spare = spare - more
    return np.array(given)


def normal_values(stream_key, shape, scale, most, cuts=(), kind=jnp.bfloat16):
    loudness = block_levels(stream_key, shape, cuts, -0.22, 0.18) if cuts else 1.0
    array = jax.random.normal(stream_key, shape, jnp.float32) * scale * loudness
    return jnp.minimum(jnp.maximum(array, -most), most).astype(kind)


def setup_inputs(seed: int = 0) -> dict:
    splits = jax.random.split(jax.random.key(seed), 10)
    columns = draw_columns(jax.random.fold_in(splits[9], 71), 0)
    leaf_of_keys = jax.random.split(jax.random.fold_in(splits[1], 1), RANK // TIME_DEV)
    leaf_of_turns = jax.random.permutation(jax.random.fold_in(splits[1], 3), RANK // TIME_DEV)
    leaf_of = jax.vmap(lambda own, number: deal_out(jax.random.fold_in(splits[1], 2), own, number, TIME_DEV, LEAVES, 1, M, 2))(leaf_of_keys, leaf_of_turns).reshape((RANK, 1))
    inverse_root = draw_inverse_root(jax.random.fold_in(splits[9], 71), 0)
    inverse_upper = draw_inverse_upper(jax.random.fold_in(splits[9], 71), 0)
    inverse_middle = draw_inverse_middle(jax.random.fold_in(splits[9], 71), 0)
    inverse_leaf = draw_inverse_leaf(jax.random.fold_in(splits[9], 71), 0)
    coupling_upper = normal_values(splits[6], (UPPER_NODES * NS, 1, NS), 1.0, 6.0, ((0, 4), (2, 8)))
    coupling_middle = normal_values(splits[7], (MIDDLE_NODES * NS, 2, NS), 1.0, 6.0, ((0, 4), (2, 8)))
    coupling_leaf = normal_values(splits[8], (LEAVES * NS, 3, NS), 1.0, 6.0, ((0, 4), (2, 8)))
    return dict(columns=columns, leaf_of=leaf_of, inverse_root=inverse_root, inverse_upper=inverse_upper, inverse_middle=inverse_middle, inverse_leaf=inverse_leaf, coupling_upper=coupling_upper, coupling_middle=coupling_middle, coupling_leaf=coupling_leaf)


def route_front(columns, leaf_of):
    labels = leaf_of[:, 0].reshape(N_CUBE, TIME_DEV)
    onehot = (labels[:, :, None] == jnp.arange(LEAVES, dtype=jnp.int32)[None, None, :]).astype(jnp.int32)
    before = jnp.cumsum(onehot, axis=1, dtype=jnp.int32) - onehot
    within = jnp.sum(before * onehot, axis=2, dtype=jnp.int32)
    sender = jnp.arange(N_CUBE, dtype=jnp.int32)[:, None]
    destination = (labels * LEAF_SPAN + within // PER_SLOT) * C_DEV + sender * PER_SLOT + within % PER_SLOT
    empty = jnp.zeros((FRONT, 4, NS), jnp.bfloat16)
    return empty.at[destination.reshape(-1).astype(jnp.int32)].set(columns)

def reference(columns, leaf_of, inverse_root, inverse_upper, inverse_middle, inverse_leaf, coupling_upper, coupling_middle, coupling_leaf):
    front_cols = route_front(columns, leaf_of)
    inverses = (inverse_root, inverse_upper, inverse_middle, inverse_leaf)
    couplings = (None, coupling_upper, coupling_middle, coupling_leaf)
    results = [None, None, None, None]
    factor = None
    for tree_level in (3, 2, 1, 0):
        node_count = min(2 ** tree_level, N_CUBE)
        group_width = FRONT // node_count
        pieces = []
        fronts = []
        for node in range(node_count):
            block_cols = front_cols[node * group_width:(node + 1) * group_width]
            inverse = inverses[tree_level][node * NS:(node + 1) * NS]
            projected = jnp.dot(inverse.astype(jnp.float32), block_cols[:, 0, :].T.astype(jnp.float32), preferred_element_type=jnp.float32).astype(jnp.bfloat16)
            gram_local = jnp.dot(projected.T.astype(jnp.float32), projected.astype(jnp.float32), preferred_element_type=jnp.float32)
            factor = jnp.linalg.cholesky(jnp.eye(group_width, dtype=jnp.float32) + gram_local)
            pieces.append(projected)
            if tree_level > 0:
                coupling = couplings[tree_level][node * NS:(node + 1) * NS].reshape(NS, tree_level * NS)
                cross_term = jnp.dot(projected.T.astype(jnp.float32), coupling.astype(jnp.float32), preferred_element_type=jnp.float32)
                remainder = block_cols[:, 1:, :].reshape(group_width, tree_level * NS).astype(jnp.float32) - cross_term
                solved = jax.scipy.linalg.solve_triangular(factor, remainder, lower=True)
                fronts.append(solved.astype(jnp.bfloat16).reshape(group_width, tree_level, NS))
        results[tree_level] = jnp.concatenate(pieces, 0)
        if tree_level > 0:
            front_cols = jnp.concatenate(fronts, 0)
    return (factor, results[0], results[1], results[2], results[3])
```

```python
import functools

import jax
import jax.numpy as jnp
from jax import lax
from jax.experimental import pallas as pl
from jax.experimental.pallas import tpu as pltpu
from jax.sharding import PartitionSpec as P

MESH = pl.DeviceIdType.MESH
LEVELS = (3, 2, 1, 0)
SLOT = 16
NT = (((1,), (1,)), ((), ()))
NN = (((1,), (0,)), ((), ()))


def radices(size):
    steps = []
    while size > 1:
        steps.append(min(4, size))
        size //= steps[-1]
    return steps


def mm(a, b, dims):
    return lax.dot_general(a, b, dims, preferred_element_type=jnp.float32)


def mm32(a, b, dims):
    return lax.dot_general(
        a, b, dims, precision=lax.Precision.HIGHEST, preferred_element_type=jnp.float32
    )


def factor_block(block, work):
    n = block.shape[0]
    work[:, :n] = block
    row_pos = lax.broadcasted_iota(jnp.int32, (n, 128), 0)
    lane_pos = lax.broadcasted_iota(jnp.int32, (n, 128), 1)
    rows = lax.broadcasted_iota(jnp.int32, (n, 1), 0)
    m = jnp.where(lane_pos < n, work[...], 0.0) + (lane_pos == row_pos + 64).astype(jnp.float32)
    for j in range(n):
        column = jnp.where(rows > j, m[:, j : j + 1], 0.0)
        m = m - column * (m[j : j + 1, :] * (1.0 / m[j : j + 1, j : j + 1]))
    pivots = jnp.sum(jnp.where(lane_pos == row_pos, m, 0.0), axis=1, keepdims=True)
    m = m * lax.rsqrt(pivots)
    upper = jnp.where(lane_pos >= row_pos, m, 0.0)[:, :n]
    return upper, m[:, 64 : 64 + n]


def eye(n):
    return (
        lax.broadcasted_iota(jnp.int32, (n, n), 0) == lax.broadcasted_iota(jnp.int32, (n, n), 1)
    ).astype(jnp.float32)


def factor_panels(total, width, work):
    count = total.shape[0] // width
    panels = [total[k * width :, k * width : (k + 1) * width] for k in range(count)]
    result = []
    for k in range(count):
        upper, inverse = factor_block(panels[k][:width], work)
        below = None
        if k + 1 < count:
            below = mm32(panels[k][width:], inverse, NT)
            for j in range(k + 1, count):
                at = (j - k - 1) * width
                panels[j] = panels[j] - mm32(below[at:], below[at : at + width], NT)
        result.append((upper, inverse, below))
    return result


def kernel(cube, panel, width, per_slot, leaves, geometry, *refs):
    refs = list(refs)
    take = lambda count: [refs.pop(0) for _ in range(count)]
    labels, columns = take(2)
    inv_hbm = dict(zip(LEVELS, take(4)))
    coup_hbm = dict(zip(LEVELS[:3], take(3)))
    core_out = take(1)[0]
    proj_out = dict(zip(LEVELS, take(4)))
    inv = dict(zip(LEVELS, take(4)))
    coup = dict(zip(LEVELS[:3], take(3)))
    packed, arrived = take(2)
    front = dict(zip(LEVELS, take(4)))
    sent = dict(zip(LEVELS, take(4)))
    got = dict(zip(LEVELS, take(4)))
    full = dict(zip(LEVELS, take(4)))
    gram = dict(zip(LEVELS, take(4)))
    gram_part = dict(zip(LEVELS, take(4)))
    cross = dict(zip(LEVELS[:3], take(3)))
    cross_part = dict(zip(LEVELS[:3], take(3)))
    solved = dict(zip(LEVELS[:3], take(3)))
    work = take(1)[0]
    load_sem, route_send, route_recv, panel_send, panel_recv, cube_send, cube_recv = take(7)

    c = lax.axis_index("cube")
    p = lax.axis_index("panel")

    loads = {}
    for at, level in enumerate(LEVELS):
        loads[level] = [pltpu.make_async_copy(inv_hbm[level], inv[level], load_sem.at[at, 0])]
        if level:
            loads[level].append(
                pltpu.make_async_copy(coup_hbm[level], coup[level], load_sem.at[at, 1])
            )
        for load in loads[level]:
            load.start()

    barrier = pltpu.get_barrier_semaphore()

    def greet(axis, me, size):
        def one(d, carry):
            pl.semaphore_signal(
                barrier, inc=1, device_id={axis: lax.rem(me + d, size)}, device_id_type=MESH
            )
            return carry

        lax.fori_loop(1, size, one, 0)

    greet("cube", c, cube)
    greet("panel", p, panel)

    label = labels[...]
    time_cols = label.shape[1]
    share = cube // leaves
    onehot = lax.broadcasted_iota(jnp.int32, (16, time_cols), 0) == label
    earlier = lax.broadcasted_iota(jnp.int32, (time_cols, time_cols), 0) < (
        lax.broadcasted_iota(jnp.int32, (time_cols, time_cols), 1)
    )
    onehot = onehot.astype(jnp.float32)
    before = mm(onehot.astype(jnp.bfloat16), earlier.astype(jnp.float32).astype(jnp.bfloat16), NN)
    within = jnp.sum(before * onehot, axis=0, keepdims=True).astype(jnp.int32)
    turn = jnp.zeros_like(within)
    for step in range(1, share):
        turn = turn + (within >= step * per_slot).astype(jnp.int32)
    target = (label * share + turn) * SLOT + within - turn * per_slot
    dispatch = (
        (lax.broadcasted_iota(jnp.int32, (cube * SLOT, time_cols), 0) == target)
        .astype(jnp.float32)
        .astype(jnp.bfloat16)
    )
    for j in range(4):
        block = mm(dispatch, columns[j], NN).astype(jnp.bfloat16)
        packed[:, j] = block.reshape(cube, SLOT, block.shape[1])

    pl.semaphore_wait(barrier, cube + panel - 2)

    def route(d):
        to = lax.rem(c + d, cube)
        return pltpu.make_async_remote_copy(
            src_ref=packed.at[to],
            dst_ref=arrived.at[c],
            send_sem=route_send.at[d],
            recv_sem=route_recv.at[d],
            device_id={"cube": to},
            device_id_type=MESH,
        )

    def each(low, high, do):
        def one(d, carry):
            do(d)
            return carry

        lax.fori_loop(low, high, one, 0)

    each(1, cube, lambda d: route(d).start())
    arrived[c] = packed[c]
    each(1, cube, lambda d: route(d).wait_recv())
    out_pos = lax.broadcasted_iota(jnp.int32, (width, cube * SLOT), 0)
    in_pos = lax.broadcasted_iota(jnp.int32, (width, cube * SLOT), 1)
    select = jnp.zeros((width, cube * SLOT), jnp.float32)
    for s in range(cube):
        hit = (in_pos - s * SLOT == out_pos - s * per_slot) & (out_pos >= s * per_slot)
        hit = hit & (out_pos < (s + 1) * per_slot)
        select = select + hit.astype(jnp.float32)
    select = select.astype(jnp.bfloat16)
    first_size, _ = geometry[3][:2]
    first_rank = lax.rem(c, first_size)
    for j in range(4):
        mine = mm(select, arrived[:, j].reshape(cube * SLOT, arrived.shape[3]), NN)
        front[3][first_rank, j] = mine.astype(jnp.bfloat16)

    pending = []

    def settle(copy, radix):
        each(1, radix, lambda d: copy(d).wait_recv())

    def fold(slots, stage, radix):
        value = slots[stage, 0].astype(jnp.float32)
        for s in range(1, radix):
            value = value + slots[stage, s].astype(jnp.float32)
        return value

    def group_copy(level, phase, src, dst, size, d):
        rank = lax.rem(c, size)
        to = c - rank + lax.rem(rank + d, size)
        return pltpu.make_async_remote_copy(
            src_ref=src,
            dst_ref=dst,
            send_sem=cube_send.at[level, phase, d],
            recv_sem=cube_recv.at[level, phase, d],
            device_id={"cube": to},
            device_id_type=MESH,
        )

    def share_front(level, size, source):
        rank = lax.rem(c, size)
        if source is not None:
            front[level][rank] = source
        if size > 1:
            copy = lambda d: group_copy(
                level, 0, front[level].at[rank], front[level].at[rank], size, d
            )
            each(1, size, lambda d: copy(d).start())
            each(1, size, lambda d: copy(d).wait_recv())
            pending.append((1, size, copy))

    share_front(3, first_size, None)

    for at, level in enumerate(LEVELS):
        size, rows, part = geometry[level]
        wide = size * width
        rank = lax.rem(c, size)
        stripe = front[level].shape[3]
        top = front[level][:, 0].reshape(wide, stripe)
        loads[level][0].wait()

        def term(q, level=level, part=part, top=top):
            return mm(top, inv[level][pl.ds(pl.multiple_of(q * part, part), part), :], NT)

        def scatter(d, level=level):
            to = lax.rem(p + d, panel)
            return pltpu.make_async_remote_copy(
                src_ref=sent[level].at[d],
                dst_ref=got[level].at[d],
                send_sem=panel_send.at[level, 0, d],
                recv_sem=panel_recv.at[level, 0, d],
                device_id={"panel": to},
                device_id_type=MESH,
            )

        def send_term(d, level=level, term=term, scatter=scatter):
            sent[level][d] = term(lax.rem(p + d, panel)).astype(jnp.bfloat16)
            scatter(d).start()

        each(1, panel, send_term)
        own = term(p)
        for d in range(1, panel):
            scatter(d).wait_recv()
            own = own + got[level][d].astype(jnp.float32)
        own = own.astype(jnp.bfloat16)
        proj_out[level][...] = own
        full[level][p] = own

        def gather(d, level=level):
            to = lax.rem(p + d, panel)
            return pltpu.make_async_remote_copy(
                src_ref=full[level].at[p],
                dst_ref=full[level].at[p],
                send_sem=panel_send.at[level, 1, d],
                recv_sem=panel_recv.at[level, 1, d],
                device_id={"panel": to},
                device_id_type=MESH,
            )

        each(1, panel, lambda d, gather=gather: gather(d).start())
        pending.append((1, panel, scatter))
        pending.append((1, panel, gather))

        if level:
            loads[level][1].wait()

        def add_chunk(q, first, level=level, part=part):
            chunk = full[level][q]
            value = mm(chunk, chunk, NT)
            gram[level][...] = value if first else gram[level][...] + value
            for j in range(level):
                block = coup[level][j, pl.ds(pl.multiple_of(q * part, part), part), :]
                value = mm(chunk, block, NN)
                cross[level][j] = value if first else cross[level][j] + value

        add_chunk(p, True)

        def receive(d, gather=gather, add_chunk=add_chunk):
            gather(d).wait_recv()
            add_chunk(lax.rem(p + panel - d, panel), False)

        each(1, panel, receive)

        steps = radices(size)
        stride = 1
        copies = None
        for stage, radix in enumerate(steps):
            if stage and level:
                settle(copies[1], radix_before)
                cross[level][...] = fold(cross_part[level], stage - 1, radix_before)
            digit = lax.rem(lax.div(rank, stride), radix)
            copies = []
            for kind, slots, acc in ((0, gram_part, gram), (1, cross_part, cross)):
                if kind and not level:
                    continue
                slots[level][stage, digit] = acc[level][...].astype(slots[level].dtype)

                def copy(d, kind=kind, slot=slots[level], stage=stage, digit=digit, stride=stride, radix=radix, level=level):
                    return pltpu.make_async_remote_copy(
                        src_ref=slot.at[stage, digit],
                        dst_ref=slot.at[stage, digit],
                        send_sem=cube_send.at[level, 1 + 2 * stage + kind, d],
                        recv_sem=cube_recv.at[level, 1 + 2 * stage + kind, d],
                        device_id={"cube": c + (lax.rem(digit + d, radix) - digit) * stride},
                        device_id_type=MESH,
                    )

                each(1, radix, lambda d, copy=copy: copy(d).start())
                pending.append((1, radix, copy))
                copies.append(copy)
            settle(copies[0], radix)
            gram[level][...] = fold(gram_part[level], stage, radix)
            radix_before, stride = radix, stride * radix
        total = eye(wide) + gram[level][...]
        blocks = factor_panels(total, width, work)
        if not level:
            for k, (upper, _, below) in enumerate(blocks):
                low = k * width
                if k:
                    core_out[:low, low : low + width] = jnp.zeros((low, width), jnp.float32)
                core_out[low : low + width, low : low + width] = mm32(eye(width), upper, NT)
                if below is not None:
                    core_out[low + width :, low : low + width] = below
            break
        if steps:
            settle(copies[1], radix_before)
            summed_all = fold(cross_part[level], len(steps) - 1, radix_before)
        for j in range(level):
            summed = summed_all[j] if steps else cross[level][j]
            for k, (_, inverse, below) in enumerate(blocks):
                low = k * width
                right = front[level][k, j + 1].astype(jnp.float32) - summed[low : low + width]
                for earlier_k in range(k):
                    at_row = (k - earlier_k - 1) * width
                    right = right - mm32(
                        blocks[earlier_k][2][at_row : at_row + width], values[earlier_k], NN
                    )
                values = [] if k == 0 else values
                values.append(mm32(inverse, right, NN))
                solved[level][k, j] = values[k].astype(jnp.bfloat16)
        share_front(level - 1, geometry[level - 1][0], solved[level][rank])

    each(1, cube, lambda d: route(d).wait_send())
    for low, high, copy in pending:
        each(low, high, lambda d, copy=copy: copy(d).wait_send())


def body(
    cube,
    panel,
    columns,
    leaf_of,
    inverse_root,
    inverse_upper,
    inverse_middle,
    inverse_leaf,
    coupling_upper,
    coupling_middle,
    coupling_leaf,
):
    time_cols, _, stripe = columns.shape
    leaves = min(8, cube)
    leaf_share = cube // leaves
    per_slot = max(1, (2 * time_cols // leaves + leaf_share - 1) // leaf_share)
    width = cube * per_slot
    inverses = [inverse_leaf, inverse_middle, inverse_upper, inverse_root]
    couplings = [
        jnp.transpose(x, (1, 0, 2)) for x in (coupling_leaf, coupling_middle, coupling_upper)
    ]
    geometry = {}
    for level, inverse in zip(LEVELS, inverses):
        rows = inverse.shape[0]
        geometry[level] = (cube // min(2**level, cube), rows, rows // panel)
    wide = {level: geometry[level][0] * width for level in LEVELS}
    part = {level: geometry[level][2] for level in LEVELS}
    size = {level: geometry[level][0] for level in LEVELS}
    vm = pltpu.VMEM
    scratch = [vm(x.shape, x.dtype) for x in inverses]
    scratch += [vm(x.shape, x.dtype) for x in couplings]
    scratch += [vm((cube, 4, SLOT, stripe), jnp.bfloat16)] * 2
    scratch += [vm((size[l], l + 1, width, stripe), jnp.bfloat16) for l in LEVELS]
    for _ in range(3):
        scratch += [vm((panel, wide[l], part[l]), jnp.bfloat16) for l in LEVELS]
    scratch += [vm((wide[l], wide[l]), jnp.float32) for l in LEVELS]
    for l in LEVELS:
        steps = radices(size[l]) or [1]
        kind = jnp.float32 if size[l] <= 4 else jnp.bfloat16
        scratch += [vm((len(steps), max(steps), wide[l], wide[l]) if size[l] > 1 else (1, 1, 8, 128), kind)]
    scratch += [vm((l, wide[l], stripe), jnp.float32) for l in LEVELS[:3]]
    for l in LEVELS[:3]:
        steps = radices(size[l]) or [1]
        scratch += [vm((len(steps), max(steps), l, wide[l], stripe), jnp.bfloat16)]
    scratch += [vm((size[l], l, width, stripe), jnp.bfloat16) for l in LEVELS[:3]]
    scratch += [vm((width, 128), jnp.float32)]
    dma = pltpu.SemaphoreType.DMA
    scratch += [dma((4, 2)), dma((cube,)), dma((cube,)), dma((4, 2, panel)), dma((4, 2, panel))]
    scratch += [dma((4, 5, cube)), dma((4, 5, cube))]
    outs = [jax.ShapeDtypeStruct((wide[0], wide[0]), jnp.float32)]
    outs += [jax.ShapeDtypeStruct((wide[l], part[l]), jnp.bfloat16) for l in LEVELS]
    in_vmem = pl.BlockSpec(memory_space=pltpu.VMEM)
    in_any = pl.BlockSpec(memory_space=pl.ANY)
    core, leaf, middle, upper, root = pl.pallas_call(
        functools.partial(kernel, cube, panel, width, per_slot, leaves, geometry),
        out_shape=outs,
        in_specs=[in_vmem, in_vmem] + [in_any] * 7,
        out_specs=[in_vmem] * 5,
        scratch_shapes=scratch,
        compiler_params=pltpu.CompilerParams(
            collective_id=0, has_side_effects=True, vmem_limit_bytes=58 * 2**20
        ),
    )(
        jnp.transpose(leaf_of),
        jnp.transpose(columns, (1, 0, 2)),
        *inverses,
        *couplings,
    )
    return (core, root.T, upper.T, middle.T, leaf.T)


def solution(mesh):
    in_specs = (
        P("cube", None, "panel"),
        P("cube", None),
        P("cube", "panel"),
        P("cube", "panel"),
        P("cube", "panel"),
        P("cube", "panel"),
        P("cube", None, "panel"),
        P("cube", None, "panel"),
        P("cube", None, "panel"),
    )
    out_specs = (
        P(),
        P(("cube", "panel"), None),
        P(("cube", "panel"), None),
        P(("cube", "panel"), None),
        P(("cube", "panel"), None),
    )
    run = functools.partial(body, mesh.shape["cube"], mesh.shape["panel"])
    return jax.shard_map(run, mesh=mesh, in_specs=in_specs, out_specs=out_specs, check_vma=False)
```

```python
import functools

import jax
import jax.numpy as jnp
from jax import lax
from jax.experimental import pallas as pl
from jax.experimental.pallas import tpu as pltpu
from jax.sharding import PartitionSpec as P

MESH = pl.DeviceIdType.MESH
LEVELS = (3, 2, 1, 0)
SLOT = 16
NT = (((1,), (1,)), ((), ()))
NN = (((1,), (0,)), ((), ()))


def radices(size):
    steps = []
    while size > 1:
        steps.append(min(4, size))
        size //= steps[-1]
    return steps


def mm(a, b, dims):
    return lax.dot_general(a, b, dims, preferred_element_type=jnp.float32)


def mm32(a, b, dims):
    return lax.dot_general(
        a, b, dims, precision=lax.Precision.HIGHEST, preferred_element_type=jnp.float32
    )


def factor_block(block, work):
    n = block.shape[0]
    work[:, :n] = block
    row_pos = lax.broadcasted_iota(jnp.int32, (n, 128), 0)
    lane_pos = lax.broadcasted_iota(jnp.int32, (n, 128), 1)
    m = jnp.where(lane_pos < n, work[...], 0.0) + (lane_pos == row_pos + 64).astype(jnp.float32)
    done = []
    for j in range(0, n, 2):
        if j and j % 8 == 0:
            done.append(m[:8])
            m = m[8:]
        at = j % 8
        shape = m.shape
        here = row_pos[: shape[0]]
        first = jnp.broadcast_to(m[:, j : j + 1], shape)
        second = jnp.broadcast_to(m[:, j + 1 : j + 2], shape)
        a, b, d = first[at : at + 1], first[at + 1 : at + 2], second[at + 1 : at + 2]
        over_a, over_d = 1.0 / a, a * (1.0 / (a * d - b * b))
        ratio = b * over_a
        top, next_row = m[at : at + 1], m[at + 1 : at + 2]
        low = jnp.where(here > at + 1, second - ratio * first, 0.0)
        first = jnp.where(here > at, first, 0.0)
        m = m - first * (top * over_a) - low * ((next_row - ratio * top) * over_d)
    m = jnp.concatenate(done + [m], axis=0)
    pivots = jnp.sum(jnp.where(lane_pos == row_pos, m, 0.0), axis=1, keepdims=True)
    m = m * lax.rsqrt(pivots)
    upper = jnp.where(lane_pos >= row_pos, m, 0.0)[:, :n]
    return upper, m[:, 64 : 64 + n]


def eye(n):
    return (
        lax.broadcasted_iota(jnp.int32, (n, n), 0) == lax.broadcasted_iota(jnp.int32, (n, n), 1)
    ).astype(jnp.float32)


def factor_panels(total, width, work):
    count = total.shape[0] // width
    panels = [total[k * width :, k * width : (k + 1) * width] for k in range(count)]
    result = []
    for k in range(count):
        upper, inverse = factor_block(panels[k][:width], work)
        below = None
        if k + 1 < count:
            below = mm32(panels[k][width:], inverse, NT)
            for j in range(k + 1, count):
                at = (j - k - 1) * width
                panels[j] = panels[j] - mm32(below[at:], below[at : at + width], NT)
        result.append((upper, inverse, below))
    return result


def kernel(cube, panel, width, per_slot, leaves, geometry, *refs):
    refs = list(refs)
    take = lambda count: [refs.pop(0) for _ in range(count)]
    labels, columns = take(2)
    inv_hbm = dict(zip(LEVELS, take(4)))
    coup_hbm = dict(zip(LEVELS[:3], take(3)))
    core_out = take(1)[0]
    proj_out = dict(zip(LEVELS, take(4)))
    inv = dict(zip(LEVELS, take(4)))
    coup = dict(zip(LEVELS[:3], take(3)))
    packed, arrived = take(2)
    front = dict(zip(LEVELS, take(4)))
    twin_sent = dict(zip(LEVELS, take(4)))
    twin_got = dict(zip(LEVELS, take(4)))
    sent = dict(zip(LEVELS, take(4)))
    got = dict(zip(LEVELS, take(4)))
    full = dict(zip(LEVELS, take(4)))
    gram = dict(zip(LEVELS, take(4)))
    gram_part = dict(zip(LEVELS, take(4)))
    cross = dict(zip(LEVELS[:3], take(3)))
    cross_part = dict(zip(LEVELS[:3], take(3)))
    solved = dict(zip(LEVELS[:3], take(3)))
    work = take(1)[0]
    load_sem, route_send, route_recv, panel_send, panel_recv, cube_send, cube_recv = take(7)

    c = lax.axis_index("cube")
    p = lax.axis_index("panel")
    chips = panel // 2
    chip, core = lax.div(p, 2), lax.rem(p, 2)

    loads = {}
    for at, level in enumerate(LEVELS):
        loads[level] = [pltpu.make_async_copy(inv_hbm[level], inv[level], load_sem.at[at, 0])]
        if level:
            loads[level].append(
                pltpu.make_async_copy(coup_hbm[level], coup[level], load_sem.at[at, 1])
            )
        for load in loads[level]:
            load.start()

    barrier = pltpu.get_barrier_semaphore()

    def greet(axis, me, size):
        def one(d, carry):
            pl.semaphore_signal(
                barrier, inc=1, device_id={axis: lax.rem(me + d, size)}, device_id_type=MESH
            )
            return carry

        lax.fori_loop(1, size, one, 0)

    greet("cube", c, cube)
    greet("panel", p, panel)

    label = labels[...]
    time_cols = label.shape[1]
    share = cube // leaves
    onehot = lax.broadcasted_iota(jnp.int32, (16, time_cols), 0) == label
    earlier = lax.broadcasted_iota(jnp.int32, (time_cols, time_cols), 0) < (
        lax.broadcasted_iota(jnp.int32, (time_cols, time_cols), 1)
    )
    onehot = onehot.astype(jnp.float32)
    before = mm(onehot.astype(jnp.bfloat16), earlier.astype(jnp.float32).astype(jnp.bfloat16), NN)
    within = jnp.sum(before * onehot, axis=0, keepdims=True).astype(jnp.int32)
    turn = jnp.zeros_like(within)
    for step in range(1, share):
        turn = turn + (within >= step * per_slot).astype(jnp.int32)
    target = (label * share + turn) * SLOT + within - turn * per_slot
    dispatch = (
        (lax.broadcasted_iota(jnp.int32, (cube * SLOT, time_cols), 0) == target)
        .astype(jnp.float32)
        .astype(jnp.bfloat16)
    )
    for j in range(4):
        block = mm(dispatch, columns[j], NN).astype(jnp.bfloat16)
        packed[:, j] = block.reshape(cube, SLOT, block.shape[1])

    pl.semaphore_wait(barrier, cube + panel - 2)

    def route(d):
        to = lax.rem(c + d, cube)
        return pltpu.make_async_remote_copy(
            src_ref=packed.at[to],
            dst_ref=arrived.at[c],
            send_sem=route_send.at[d],
            recv_sem=route_recv.at[d],
            device_id={"cube": to},
            device_id_type=MESH,
        )

    def each(low, high, do):
        def one(d, carry):
            do(d)
            return carry

        lax.fori_loop(low, high, one, 0)

    each(1, cube, lambda d: route(d).start())
    arrived[c] = packed[c]
    each(1, cube, lambda d: route(d).wait_recv())
    out_pos = lax.broadcasted_iota(jnp.int32, (width, cube * SLOT), 0)
    in_pos = lax.broadcasted_iota(jnp.int32, (width, cube * SLOT), 1)
    select = jnp.zeros((width, cube * SLOT), jnp.float32)
    for s in range(cube):
        hit = (in_pos - s * SLOT == out_pos - s * per_slot) & (out_pos >= s * per_slot)
        hit = hit & (out_pos < (s + 1) * per_slot)
        select = select + hit.astype(jnp.float32)
    select = select.astype(jnp.bfloat16)
    first_size, _ = geometry[3][:2]
    first_rank = lax.rem(c, first_size)
    for j in range(4):
        mine = mm(select, arrived[:, j].reshape(cube * SLOT, arrived.shape[3]), NN)
        front[3][first_rank, j] = mine.astype(jnp.bfloat16)

    pending = []

    def settle(copy, radix):
        each(1, radix, lambda d: copy(d).wait_recv())

    def fold(slots, stage, radix):
        value = slots[stage, 0].astype(jnp.float32)
        for s in range(1, radix):
            value = value + slots[stage, s].astype(jnp.float32)
        return value

    def group_copy(level, phase, src, dst, size, d):
        rank = lax.rem(c, size)
        to = c - rank + lax.rem(rank + d, size)
        return pltpu.make_async_remote_copy(
            src_ref=src,
            dst_ref=dst,
            send_sem=cube_send.at[level, phase, d],
            recv_sem=cube_recv.at[level, phase, d],
            device_id={"cube": to},
            device_id_type=MESH,
        )

    def share_front(level, size, source):
        rank = lax.rem(c, size)
        if source is not None:
            front[level][rank] = source
        if size > 1:
            copy = lambda d: group_copy(
                level, 0, front[level].at[rank], front[level].at[rank], size, d
            )
            each(1, size, lambda d: copy(d).start())
            each(1, size, lambda d: copy(d).wait_recv())
            pending.append((1, size, copy))

    share_front(3, first_size, None)

    for at, level in enumerate(LEVELS):
        size, rows, part = geometry[level]
        wide = size * width
        rank = lax.rem(c, size)
        stripe = front[level].shape[3]
        top = front[level][:, 0].reshape(wide, stripe)
        loads[level][0].wait()

        def term(z, core, level=level, part=part, top=top):
            at_row = pl.multiple_of((2 * z + core) * part, part)
            return mm(top, inv[level][pl.ds(at_row, part), :], NT)

        def panel_copy(kind, src, dst, d, z, core, level=level):
            return pltpu.make_async_remote_copy(
                src_ref=src,
                dst_ref=dst,
                send_sem=panel_send.at[level, kind, d],
                recv_sem=panel_recv.at[level, kind, d],
                device_id={"panel": 2 * z + core},
                device_id_type=MESH,
            )

        def to_twin(d, level=level, panel_copy=panel_copy):
            return panel_copy(0, twin_sent[level].at[d], twin_got[level].at[d], d, chip, 1 - core)

        def scatter(d, level=level, panel_copy=panel_copy):
            to = lax.rem(chip + d, chips)
            return panel_copy(1, sent[level].at[d], got[level].at[d], d, to, core)

        def send_twin(d, level=level, term=term, to_twin=to_twin):
            twin_sent[level][d] = term(lax.rem(chip + d, chips), 1 - core).astype(jnp.bfloat16)
            to_twin(d).start()

        def send_term(d, level=level, term=term, to_twin=to_twin, scatter=scatter):
            mine = term(lax.rem(chip + d, chips), core)
            to_twin(d).wait_recv()
            sent[level][d] = (mine + twin_got[level][d].astype(jnp.float32)).astype(jnp.bfloat16)
            scatter(d).start()

        each(1, chips, send_twin)
        send_twin(0)
        each(1, chips, send_term)
        own = term(chip, core)
        to_twin(0).wait_recv()
        own = own + twin_got[level][0].astype(jnp.float32)
        for d in range(1, chips):
            scatter(d).wait_recv()
            own = own + got[level][d].astype(jnp.float32)
        own = own.astype(jnp.bfloat16)
        full[level][chip, core] = own

        def gather(d, level=level, panel_copy=panel_copy):
            here = full[level].at[chip, core]
            return panel_copy(2, here, here, d, lax.rem(chip + d, chips), core)

        def forward(d, level=level, panel_copy=panel_copy):
            here = full[level].at[lax.rem(chip + chips - d, chips), core]
            return panel_copy(3, here, here, d, chip, 1 - core)

        each(1, chips, lambda d, gather=gather: gather(d).start())
        forward(0).start()
        proj_out[level][...] = own
        pending.append((0, chips, to_twin))
        pending.append((1, chips, scatter))
        pending.append((1, chips, gather))
        pending.append((0, chips, forward))

        if level:
            loads[level][1].wait()

        def add_chunk(z, core, first, level=level, part=part):
            chunk = full[level][z, core]
            value = mm(chunk, chunk, NT)
            gram[level][...] = value if first else gram[level][...] + value
            for j in range(level):
                at_row = pl.multiple_of((2 * z + core) * part, part)
                value = mm(chunk, coup[level][j, pl.ds(at_row, part), :], NN)
                cross[level][j] = value if first else cross[level][j] + value

        add_chunk(chip, core, True)

        def receive(d, gather=gather, forward=forward, add_chunk=add_chunk):
            gather(d).wait_recv()
            forward(d).start()
            add_chunk(lax.rem(chip + chips - d, chips), core, False)

        def receive_twin(d, forward=forward, add_chunk=add_chunk):
            forward(d).wait_recv()
            add_chunk(lax.rem(chip + chips - d, chips), 1 - core, False)

        each(1, chips, receive)
        each(0, chips, receive_twin)

        steps = radices(size)
        stride = 1
        copies = None
        for stage, radix in enumerate(steps):
            if stage and level:
                settle(copies[1], radix_before)
                cross[level][...] = fold(cross_part[level], stage - 1, radix_before)
            digit = lax.rem(lax.div(rank, stride), radix)
            copies = []
            for kind, slots, acc in ((0, gram_part, gram), (1, cross_part, cross)):
                if kind and not level:
                    continue
                slots[level][stage, digit] = acc[level][...].astype(slots[level].dtype)

                def copy(d, kind=kind, slot=slots[level], stage=stage, digit=digit, stride=stride, radix=radix, level=level):
                    return pltpu.make_async_remote_copy(
                        src_ref=slot.at[stage, digit],
                        dst_ref=slot.at[stage, digit],
                        send_sem=cube_send.at[level, 1 + 2 * stage + kind, d],
                        recv_sem=cube_recv.at[level, 1 + 2 * stage + kind, d],
                        device_id={"cube": c + (lax.rem(digit + d, radix) - digit) * stride},
                        device_id_type=MESH,
                    )

                each(1, radix, lambda d, copy=copy: copy(d).start())
                pending.append((1, radix, copy))
                copies.append(copy)
            settle(copies[0], radix)
            gram[level][...] = fold(gram_part[level], stage, radix)
            radix_before, stride = radix, stride * radix
        total = eye(wide) + gram[level][...]
        blocks = factor_panels(total, width, work)
        if not level:
            for k, (upper, _, below) in enumerate(blocks):
                low = k * width
                if k:
                    core_out[:low, low : low + width] = jnp.zeros((low, width), jnp.float32)
                core_out[low : low + width, low : low + width] = mm32(eye(width), upper, NT)
                if below is not None:
                    core_out[low + width :, low : low + width] = below
            break
        if steps:
            settle(copies[1], radix_before)
            summed_all = fold(cross_part[level], len(steps) - 1, radix_before)
        for j in range(level):
            summed = summed_all[j] if steps else cross[level][j]
            for k, (_, inverse, below) in enumerate(blocks):
                low = k * width
                right = front[level][k, j + 1].astype(jnp.float32) - summed[low : low + width]
                for earlier_k in range(k):
                    at_row = (k - earlier_k - 1) * width
                    right = right - mm32(
                        blocks[earlier_k][2][at_row : at_row + width], values[earlier_k], NN
                    )
                values = [] if k == 0 else values
                values.append(mm32(inverse, right, NN))
                solved[level][k, j] = values[k].astype(jnp.bfloat16)
        share_front(level - 1, geometry[level - 1][0], solved[level][rank])

    each(1, cube, lambda d: route(d).wait_send())
    for low, high, copy in pending:
        each(low, high, lambda d, copy=copy: copy(d).wait_send())


def hand_out(*refs):
    for source, result in zip(refs[:5], refs[5:]):
        result[...] = source[...]


def body(
    cube,
    panel,
    columns,
    leaf_of,
    inverse_root,
    inverse_upper,
    inverse_middle,
    inverse_leaf,
    coupling_upper,
    coupling_middle,
    coupling_leaf,
):
    time_cols, _, stripe = columns.shape
    leaves = min(8, cube)
    leaf_share = cube // leaves
    per_slot = max(1, (2 * time_cols // leaves + leaf_share - 1) // leaf_share)
    width = cube * per_slot
    inverses = [inverse_leaf, inverse_middle, inverse_upper, inverse_root]
    couplings = [
        jnp.transpose(x, (1, 0, 2)) for x in (coupling_leaf, coupling_middle, coupling_upper)
    ]
    geometry = {}
    for level, inverse in zip(LEVELS, inverses):
        rows = inverse.shape[0]
        geometry[level] = (cube // min(2**level, cube), rows, rows // panel)
    wide = {level: geometry[level][0] * width for level in LEVELS}
    part = {level: geometry[level][2] for level in LEVELS}
    size = {level: geometry[level][0] for level in LEVELS}
    vm = pltpu.VMEM
    scratch = [vm(x.shape, x.dtype) for x in inverses]
    scratch += [vm(x.shape, x.dtype) for x in couplings]
    scratch += [vm((cube, 4, SLOT, stripe), jnp.bfloat16)] * 2
    scratch += [vm((size[l], l + 1, width, stripe), jnp.bfloat16) for l in LEVELS]
    for _ in range(4):
        scratch += [vm((panel // 2, wide[l], part[l]), jnp.bfloat16) for l in LEVELS]
    scratch += [vm((panel // 2, 2, wide[l], part[l]), jnp.bfloat16) for l in LEVELS]
    scratch += [vm((wide[l], wide[l]), jnp.float32) for l in LEVELS]
    for l in LEVELS:
        steps = radices(size[l]) or [1]
        kind = jnp.float32 if size[l] <= 4 else jnp.bfloat16
        scratch += [vm((len(steps), max(steps), wide[l], wide[l]) if size[l] > 1 else (1, 1, 8, 128), kind)]
    scratch += [vm((l, wide[l], stripe), jnp.float32) for l in LEVELS[:3]]
    for l in LEVELS[:3]:
        steps = radices(size[l]) or [1]
        scratch += [vm((len(steps), max(steps), l, wide[l], stripe), jnp.bfloat16)]
    scratch += [vm((size[l], l, width, stripe), jnp.bfloat16) for l in LEVELS[:3]]
    scratch += [vm((width, 128), jnp.float32)]
    dma = pltpu.SemaphoreType.DMA
    scratch += [dma((4, 2)), dma((cube,)), dma((cube,)), dma((4, 4, panel // 2)), dma((4, 4, panel // 2))]
    scratch += [dma((4, 5, cube)), dma((4, 5, cube))]
    outs = [jax.ShapeDtypeStruct((wide[0], wide[0]), jnp.float32)]
    outs += [jax.ShapeDtypeStruct((wide[l], part[l]), jnp.bfloat16) for l in LEVELS]
    in_vmem = pl.BlockSpec(memory_space=pltpu.VMEM)
    in_any = pl.BlockSpec(memory_space=pl.ANY)
    core, leaf, middle, upper, root = pl.pallas_call(
        functools.partial(kernel, cube, panel, width, per_slot, leaves, geometry),
        out_shape=outs,
        in_specs=[in_vmem, in_vmem] + [in_any] * 7,
        out_specs=[in_vmem] * 5,
        scratch_shapes=scratch,
        compiler_params=pltpu.CompilerParams(
            collective_id=0, has_side_effects=True, vmem_limit_bytes=58 * 2**20
        ),
    )(
        jnp.transpose(leaf_of),
        jnp.transpose(columns, (1, 0, 2)),
        *inverses,
        *couplings,
    )
    core, leaf, middle, upper, root = pl.pallas_call(
        hand_out,
        out_shape=outs,
        in_specs=[in_vmem] * 5,
        out_specs=[in_vmem] * 5,
    )(core, leaf, middle, upper, root)
    return (core, root.T, upper.T, middle.T, leaf.T)


def solution(mesh):
    in_specs = (
        P("cube", None, "panel"),
        P("cube", None),
        P("cube", "panel"),
        P("cube", "panel"),
        P("cube", "panel"),
        P("cube", "panel"),
        P("cube", None, "panel"),
        P("cube", None, "panel"),
        P("cube", None, "panel"),
    )
    out_specs = (
        P(),
        P(("cube", "panel"), None),
        P(("cube", "panel"), None),
        P(("cube", "panel"), None),
        P(("cube", "panel"), None),
    )
    run = functools.partial(body, mesh.shape["cube"], mesh.shape["panel"])
    return jax.shard_map(run, mesh=mesh, in_specs=in_specs, out_specs=out_specs, check_vma=False)
```
